32 devices in a mesh: grp: 2 (over y), seq: 4 (over z), batch: 4 (over x, core).
Axes of the slice: x: 2, y: 2, z: 4, core: 2. Of those that a mesh axis runs over, the one named last changes fastest.
Arguments:
- head_split_gradient: bfloat16 [8, 768, 2048], P(('grp', 'batch'), 'seq'), parts along dimension 0, may hold values from -6 to 6
- first_layer_input: bfloat16 [8, 768, 2048], P(('grp', 'batch'), None, 'seq'), parts along dimension 0, may hold values from -40 to 40
- second_layer_input: bfloat16 [8, 768, 2048], P(('grp', 'batch'), None, 'seq'), parts along dimension 0, may hold values from -40 to 40
- first_layer_weight: bfloat16 [3, 768, 768], replicated, may hold values from -0.125 to 0.125
- second_layer_weight: bfloat16 [3, 768, 768], replicated, may hold values from -0.125 to 0.125
- first_norm_gain: float32 [768], replicated, may hold values from 0.1 to 1.9
- second_norm_gain: float32 [768], replicated, may hold values from 0.1 to 1.9
Outputs:
- input_gradient_total: bfloat16 [8, 768, 2048], P(('grp', 'batch'), None, 'seq'), parts along dimension 0
- first_weight_gradient: float32 [4608, 768], P(('grp', 'seq')), parts along dimension 0
The draws below stay inside these ranges and needn't reach their ends.
There are 2 independent parts, one for each index of `grp`. The reference program is written for one: setup_inputs(seed, part) draws one part's arguments, and reference() takes and returns one part's arrays. A program takes and returns all parts, laid end to end along the dimension named above; an argument that names none is the same for every part. Nothing has to cross between parts.
All inputs are finite; a program needn't handle non-finite values.
Results may differ from the reference program's by a relative error of at most 0.005.
Values may be sent and summed in bfloat16 or wider, within the bound.
No kernel may reach another device: no remote copies, remote signals or barrier semaphores. Data moves between devices by JAX's collectives and lax.ppermute only.
A program may use at most 64 MiB of HBM per device.

```python
import math
import jax
import jax.numpy as jnp
from jax import lax

C = 768
DILATION_FIRST = 512
DILATION_SECOND = 1024
BATCH = 4
POS = 2048


def draw_activation(key):
    key_base, key_pos, key_chan = jax.random.split(key, 3)
    base = jax.random.normal(key_base, (BATCH, C, POS), jnp.float32)
    lowest, highest = (0.3, 3.0)
    pos_scale = jnp.exp(jax.random.uniform(key_pos, (BATCH, 1, POS), jnp.float32, math.log(lowest), math.log(highest)))
    chan_scale = jnp.exp(jax.random.uniform(key_chan, (1, C, 1), jnp.float32, math.log(lowest), math.log(highest)))
    return jnp.clip(base * pos_scale * chan_scale, -40.0, 40.0).astype(jnp.bfloat16)


def draw_first_layer_input(key, part):
    return draw_activation(jax.random.fold_in(key, 11))


def draw_second_layer_input(key, part):
    return draw_activation(jax.random.fold_in(key, 23))


def steps_of(stream_key, extent, shards, low, largest):
    gain, own = 1.0, jax.random.fold_in(stream_key, 6)
    for dim, shards_of in shards:
        draws = jnp.exp(jax.random.uniform(jax.random.fold_in(own, dim), (shards_of,), jnp.float32, low / len(shards), largest / len(shards)))
        gain = gain * jnp.repeat(draws, extent[dim] // shards_of).reshape([-1 if axis == dim else 1 for axis in range(len(extent))])
    return gain


def noise(key, dims, width, limit, cuts=(), held_as=jnp.bfloat16):
    values = jax.random.normal(key, dims, jnp.float32) * width
    if len(cuts) > 0:
        values = steps_of(key, dims, cuts, -0.22, 0.18) * values
    return jnp.clip(values, min=-limit, max=limit).astype(held_as)


def setup_inputs(seed: int = 0, part: int = 0) -> dict:
    seeds = jax.random.split(jax.random.key(seed), 8)
    part_splits = jax.random.split(jax.random.fold_in(seeds[7], part), 8)
    head_split_gradient = noise(part_splits[0], (BATCH, C, POS), 1.0, 6.0, ((0, 4), (1, 4)))
    first_layer_input = draw_first_layer_input(jax.random.fold_in(jax.random.fold_in(seeds[7], part), 71), part)
    second_layer_input = draw_second_layer_input(jax.random.fold_in(jax.random.fold_in(seeds[7], part), 71), part)
    first_layer_weight = noise(seeds[3], (3, C, C), (3 * C) ** -0.5, 0.125)
    second_layer_weight = noise(seeds[4], (3, C, C), (3 * C) ** -0.5, 0.125)
    first_norm_gain = jnp.clip(1.0 + 0.18 * jax.random.normal(seeds[5], (C,), jnp.float32), 0.1, 1.9)
    second_norm_gain = jnp.clip(1.0 + 0.18 * jax.random.normal(seeds[6], (C,), jnp.float32), 0.1, 1.9)
    return {"head_split_gradient": head_split_gradient, "first_layer_input": first_layer_input, "second_layer_input": second_layer_input, "first_layer_weight": first_layer_weight, "second_layer_weight": second_layer_weight, "first_norm_gain": first_norm_gain, "second_norm_gain": second_norm_gain}


EPS = 1e-06
SLOPE = math.sqrt(2.0 / math.pi)
CUBIC = 0.044715

def gelu_slope(normed):
    inner = jnp.tanh(SLOPE * (normed + CUBIC * normed * normed * normed))
    return 0.5 * (1.0 + inner) + 0.5 * normed * (1.0 - inner * inner) * SLOPE * (1.0 + 3.0 * CUBIC * normed * normed)

def prepare(inputs, gain_vec):
    xfloat = inputs.astype(jnp.float32)
    meansq = lax.optimization_barrier(jnp.mean(xfloat * xfloat, axis=1, keepdims=True))
    scale = lax.rsqrt(meansq + EPS)
    normed = xfloat * scale * gain_vec[None, :, None]
    gelu_out = jax.nn.gelu(normed, approximate=True).astype(jnp.bfloat16)
    return (xfloat, scale, normed, gelu_out)

def lower_shift(field, offset):
    return jnp.pad(field[:, :, :field.shape[2] - offset], ((0, 0), (0, 0), (offset, 0)))

def upper_shift(field, offset):
    return jnp.pad(field[:, :, offset:], ((0, 0), (0, 0), (0, offset)))

def weight_grad(g_lower, gelu_out, g_upper, grad_out, scale_factor):
    grad_float = grad_out.astype(jnp.float32)
    pieces = [jnp.einsum('bcp,bop->co', tapped.astype(jnp.float32), grad_float) for tapped in (g_lower, gelu_out, g_upper)]
    return jnp.concatenate(pieces, axis=0) * scale_factor

def input_grad(xfloat, scale, normed, gain_vec, weight, grad_out, grad_upper, grad_lower):
    wfloat = weight.astype(jnp.float32)
    dgelu = jnp.einsum('co,bop->bcp', wfloat[0], grad_upper.astype(jnp.float32))
    dgelu = dgelu + jnp.einsum('co,bop->bcp', wfloat[1], grad_out.astype(jnp.float32))
    dgelu = dgelu + jnp.einsum('co,bop->bcp', wfloat[2], grad_lower.astype(jnp.float32))
    dnorm = dgelu * gelu_slope(normed) * gain_vec[None, :, None]
    inner = lax.optimization_barrier(jnp.mean(dnorm * xfloat, axis=1, keepdims=True))
    dinput = scale * dnorm - xfloat * scale * scale * scale * inner
    return (grad_out.astype(jnp.float32) + dinput).astype(jnp.bfloat16)

def reference(head_split_gradient, first_layer_input, second_layer_input, first_layer_weight, second_layer_weight, first_norm_gain, second_norm_gain):
    scale_factor = 1.0 / math.sqrt(BATCH * POS)
    xfloat_two, scale_two, normed_two, gelu_two = prepare(second_layer_input, second_norm_gain)
    middle_gradient = input_grad(xfloat_two, scale_two, normed_two, second_norm_gain, second_layer_weight, head_split_gradient, upper_shift(head_split_gradient, DILATION_SECOND), lower_shift(head_split_gradient, DILATION_SECOND))
    xfloat_one, scale_one, normed_one, gelu_one = prepare(first_layer_input, first_norm_gain)
    input_gradient_total = input_grad(xfloat_one, scale_one, normed_one, first_norm_gain, first_layer_weight, middle_gradient, upper_shift(middle_gradient, DILATION_FIRST), lower_shift(middle_gradient, DILATION_FIRST))
    first_weight_gradient = weight_grad(lower_shift(gelu_one, DILATION_FIRST), gelu_one, upper_shift(gelu_one, DILATION_FIRST), middle_gradient, scale_factor)
    return (input_gradient_total, first_weight_gradient)
```

```python
import math

import jax
import jax.numpy as jnp
from jax import lax
from jax.experimental import pallas as pl
from jax.experimental.pallas import tpu as pltpu
from jax.sharding import PartitionSpec as P

DILATION_FIRST = 512
DILATION_SECOND = 1024


EPS = 1e-06
SLOPE = math.sqrt(2.0 / math.pi)
CUBIC = 0.044715
F32 = jnp.float32
BF16 = jnp.bfloat16


def shifted(value, axis, steps):
    count = lax.axis_size(axis)
    initial, last = (max(0, -steps), min(count, count - steps))
    return lax.ppermute(value, axis, [(source, source + steps) for source in range(initial, last)])


def gelu_slope(normed):
    inner = jnp.tanh(SLOPE * (normed + CUBIC * normed * normed * normed))
    return 0.5 * (1.0 + inner) + 0.5 * normed * (1.0 - inner * inner) * SLOPE * (
        1.0 + 3.0 * CUBIC * normed * normed
    )


def prepare(inputs, gain_vec):
    xfloat = inputs.astype(F32)
    meansq = jnp.mean(xfloat * xfloat, axis=1, keepdims=True)
    scale = lax.rsqrt(meansq + EPS)
    normed = xfloat * scale * gain_vec[None, :, None]
    gelu_out = jax.nn.gelu(normed, approximate=True).astype(BF16)
    return (xfloat, scale, normed, gelu_out)


def input_grad(xfloat, scale, normed, gain_vec, weight, grad_out, grad_upper, grad_lower):
    dgelu = jnp.einsum("co,sop->scp", weight[0], grad_upper, preferred_element_type=F32)
    dgelu = dgelu + jnp.einsum("co,sop->scp", weight[1], grad_out, preferred_element_type=F32)
    dgelu = dgelu + jnp.einsum("co,sop->scp", weight[2], grad_lower, preferred_element_type=F32)
    dnorm = dgelu * gelu_slope(normed) * gain_vec[None, :, None]
    inner = jnp.mean(dnorm * xfloat, axis=1, keepdims=True)
    dinput = scale * dnorm - xfloat * scale * scale * scale * inner
    return (grad_out.astype(F32) + dinput).astype(BF16)


def general(e_split, u_one, u_two, w_one, w_two, c_one, c_two):
    width = u_one.shape[2]
    factor = 1.0 / math.sqrt(
        u_one.shape[0] * lax.axis_size("batch") * width * lax.axis_size("seq")
    )
    e_two = lax.all_to_all(e_split, "seq", split_axis=2, concat_axis=1, tiled=True)
    span = DILATION_SECOND // width
    lower, upper = shifted(e_two, "seq", span), shifted(e_two, "seq", -span)
    xfloat, scale, normed, _ = prepare(u_two, c_two)
    e_one = input_grad(xfloat, scale, normed, c_two, w_two, e_two, upper, lower)
    span = DILATION_FIRST // width
    lower, upper = shifted(e_one, "seq", span), shifted(e_one, "seq", -span)
    xfloat, scale, normed, gelu_out = prepare(u_one, c_one)
    total = input_grad(xfloat, scale, normed, c_one, w_one, e_one, upper, lower)
    pieces = [
        jnp.einsum("scp,sop->co", gelu_out, tapped, preferred_element_type=F32)
        for tapped in (upper, e_one, lower)
    ]
    terms = jnp.concatenate(pieces, axis=0) * factor
    rows = lax.psum_scatter(terms, "seq", scatter_dimension=0, tiled=True)
    return (total, lax.psum(rows, "batch"))


def vmem():
    return pl.BlockSpec(memory_space=pltpu.VMEM)


def prep_kernel(with_gelu, u_ref, c_ref, q_ref, r_ref, *g_ref):
    u = u_ref[...].astype(F32)
    c = c_ref[...]
    r = lax.rsqrt(jnp.mean(u * u, axis=0, keepdims=True) + EPS)
    a = u * r * c
    inner = jnp.tanh(SLOPE * (a + CUBIC * a * a * a))
    slope = 0.5 * (1.0 + inner) + 0.5 * a * (1.0 - inner * inner) * SLOPE * (
        1.0 + 3.0 * CUBIC * a * a
    )
    q_ref[...] = slope * c
    r_ref[...] = r
    if with_gelu:
        g_ref[0][...] = (0.5 * a * (1.0 + inner)).astype(BF16)


def prep(u, c, with_gelu):
    chans, width = u.shape
    tile = 128
    block = pl.BlockSpec((chans, tile), lambda j: (0, j))
    shapes = [jax.ShapeDtypeStruct((chans, width), F32), jax.ShapeDtypeStruct((1, width), F32)]
    specs = [block, pl.BlockSpec((1, tile), lambda j: (0, j))]
    if with_gelu:
        shapes.append(jax.ShapeDtypeStruct((chans, width), BF16))
        specs.append(block)

    def body(*refs):
        prep_kernel(with_gelu, *refs)

    return pl.pallas_call(
        body,
        grid=(width // tile,),
        in_specs=[block, pl.BlockSpec((chans, 1), lambda j: (0, 0))],
        out_specs=specs,
        out_shape=shapes,
        cost_estimate=pl.CostEstimate(
            flops=30 * chans * width, bytes_accessed=8 * chans * width, transcendentals=chans * width
        ),
        name="prep_one" if with_gelu else "prep_two",
    )(u, c.reshape(chans, 1))


def finish(acc, e, u, q, r):
    dn = acc * q
    mean = jnp.mean(dn * u, axis=0, keepdims=True)
    return e + r * dn - u * (r * r * r * mean)


def middle(pieces, w, u, q, r, place):
    chans, width = u.shape
    part = pieces[0].shape[1]
    half = chans // 2
    tile = 256

    def body(place_ref, p0, p1, p2, p3, w_ref, u_ref, q_ref, r_ref, a_ref, b_ref, e_s, sems):
        me = place_ref[0]
        tap = place_ref[1]
        copies = []
        for k, piece in enumerate((p0, p1, p2, p3)):
            at = pl.multiple_of((me ^ k) * part, part)
            for j in range(2):
                copies.append(
                    pltpu.make_async_copy(
                        piece.at[j], e_s.at[j, pl.ds(at, part), :], sems.at[2 * k + j]
                    )
                )
        for copy in copies:
            copy.start()
        for copy in copies:
            copy.wait()
        for t in range(width // tile):
            cols = slice(t * tile, (t + 1) * tile)
            e = e_s[0, :, cols]
            acc = jnp.dot(w_ref[1], e, preferred_element_type=F32)
            acc = acc + jnp.dot(w_ref[tap], e_s[1, :, cols], preferred_element_type=F32)
            out = finish(
                acc, e.astype(F32), u_ref[:, cols].astype(F32), q_ref[:, cols], r_ref[:, cols]
            ).astype(BF16)
            a_ref[:, cols] = out[:half]
            b_ref[:, cols] = out[half:]

    return pl.pallas_call(
        body,
        in_specs=[pl.BlockSpec(memory_space=pltpu.SMEM)]
        + [pl.BlockSpec(memory_space=pl.ANY)] * 4
        + [vmem()] * 4,
        out_specs=[vmem()] * 2,
        out_shape=[jax.ShapeDtypeStruct((half, width), BF16)] * 2,
        scratch_shapes=[
            pltpu.VMEM((2, chans, width), BF16),
            pltpu.SemaphoreType.DMA((8,)),
        ],
        cost_estimate=pl.CostEstimate(
            flops=4 * chans * chans * width, bytes_accessed=10 * chans * width, transcendentals=0
        ),
        compiler_params=pltpu.CompilerParams(vmem_limit_bytes=40 << 20),
        name="middle",
    )(place, *pieces, w, u, q, r)


def taps(g, uppers, owns, lowers, place, factor, units, name):
    chans, width = g.shape
    cols = owns.shape[0]
    seq, halves = units
    unit = 3 * chans // (seq * halves * 2)
    grain = math.gcd(unit, chans)

    def body(place_ref, g_ref, up_ref, own_ref, low_ref, keep_ref, send_ref, acc_s, sem):
        core = place_ref[2]
        for tap, e_ref in enumerate((up_ref, own_ref, low_ref)):
            acc = lax.dot_general(
                g_ref[...], e_ref[...], (((1,), (1,)), ((), ())), preferred_element_type=F32
            )
            acc = acc * factor
            for j in range(chans // grain):
                row = tap * chans + j * grain
                n, off = divmod(row, unit)
                s, rest = divmod(n, 2 * halves)
                c, x = divmod(rest, halves)
                acc_s[c, x, s, off : off + grain, :] = acc[j * grain : (j + 1) * grain]
        copy = pltpu.make_async_copy(acc_s.at[core], keep_ref, sem)
        copy.start()
        send_ref[...] = acc_s[1 - core].astype(BF16)
        copy.wait()

    shape = (halves, seq, unit, cols)
    return pl.pallas_call(
        body,
        in_specs=[pl.BlockSpec(memory_space=pltpu.SMEM)] + [vmem()] * 4,
        out_specs=[pl.BlockSpec(memory_space=pl.ANY), vmem()],
        out_shape=[jax.ShapeDtypeStruct(shape, F32), jax.ShapeDtypeStruct(shape, BF16)],
        scratch_shapes=[pltpu.VMEM((2,) + shape, F32), pltpu.SemaphoreType.DMA],
        cost_estimate=pl.CostEstimate(
            flops=6 * chans * cols * width, bytes_accessed=12 * chans * cols, transcendentals=0
        ),
        compiler_params=pltpu.CompilerParams(vmem_limit_bytes=40 << 20),
        name=name,
    )(place, g, uppers, owns, lowers)


def last(uppers, owns, lowers, w, u, q, r):
    chans, width = u.shape
    half = chans // 2
    tile = 256

    def body(ua, ub, oa, ob, la, lb, w_ref, u_ref, q_ref, r_ref, out_ref):
        for t in range(width // tile):
            cols = slice(t * tile, (t + 1) * tile)
            acc = jnp.zeros((chans, tile), F32)
            for tap, (a, b) in enumerate(((ua, ub), (oa, ob), (la, lb))):
                e = jnp.concatenate([a[:, cols], b[:, cols]], axis=0)
                acc = acc + jnp.dot(w_ref[tap], e, preferred_element_type=F32)
            e = jnp.concatenate([oa[:, cols], ob[:, cols]], axis=0).astype(F32)
            out_ref[:, cols] = finish(
                acc, e, u_ref[:, cols].astype(F32), q_ref[:, cols], r_ref[:, cols]
            ).astype(BF16)

    return pl.pallas_call(
        body,
        in_specs=[vmem()] * 10,
        out_specs=vmem(),
        out_shape=jax.ShapeDtypeStruct((chans, width), BF16),
        cost_estimate=pl.CostEstimate(
            flops=6 * chans * chans * width, bytes_accessed=12 * chans * width, transcendentals=0
        ),
        compiler_params=pltpu.CompilerParams(vmem_limit_bytes=40 << 20),
        name="last",
    )(*uppers, *owns, *lowers, w, u, q, r)


def pairs(count, flip):
    return [(i, i ^ flip) for i in range(count)]


def pick(value, index):
    return lax.dynamic_index_in_dim(value, index, 0, keepdims=False)


def reduced(keep, send, seq, batch):
    core, x, me = lax.axis_index("batch") % 2, lax.axis_index("batch") // 2, lax.axis_index("seq")
    part = keep + lax.ppermute(send, "batch", pairs(batch, 1)).astype(F32)
    far = lax.ppermute(pick(part, 1 - x).astype(BF16), "batch", pairs(batch, 2))
    part = pick(part, x) + far.astype(F32)
    total = pick(part, me)
    moved = [
        lax.ppermute(pick(part, me ^ k).astype(BF16), "seq", pairs(seq, k)) for k in (3, 2, 1)
    ]
    for piece in moved:
        total = total + piece.astype(F32)
    mine = total.astype(BF16)
    other = lax.ppermute(mine, "batch", pairs(batch, 2))
    both = jnp.where(x == 0, jnp.stack([mine, other]), jnp.stack([other, mine]))
    other = lax.ppermute(both, "batch", pairs(batch, 1))
    full = jnp.where(core == 0, jnp.stack([both, other]), jnp.stack([other, both]))
    return full.astype(F32).reshape(-1, mine.shape[-1])


def four_shards(e_split, u_one, u_two, w_one, w_two, c_one, c_two):
    seq, batch = lax.axis_size("seq"), lax.axis_size("batch")
    me = lax.axis_index("seq")
    core = lax.axis_index("batch") % 2
    e_split, u_one, u_two = e_split[0], u_one[0], u_two[0]
    chans, width = u_one.shape
    part = e_split.shape[0]
    factor = 1.0 / math.sqrt(batch * width * seq)

    def block(index):
        return lax.dynamic_slice(e_split, (0, index * width), (part, width))

    pieces = [jnp.stack([block(me ^ k), block(me ^ k ^ 2)]) for k in range(4)]
    for k in (3, 2, 1):
        pieces[k] = lax.ppermute(pieces[k], "seq", pairs(seq, k))
    place = jnp.stack([me, jnp.where(me < 2, 0, 2), core]).astype(jnp.int32)
    q_two, r_two = prep(u_two, c_two, False)
    q_one, r_one, g_one = prep(u_one, c_one, True)
    owns = middle(pieces, w_two, u_two, q_two, r_two, place)
    lowers = [shifted(e, "seq", 1) for e in owns]
    uppers = [shifted(e, "seq", -1) for e in owns]
    chunks = []
    for j in range(2):
        keep, send = taps(
            g_one, uppers[j], owns[j], lowers[j], place, factor, (seq, 2), f"taps_{j}"
        )
        chunks.append(reduced(keep, send, seq, batch))
    total = last(uppers, owns, lowers, w_one, u_one, q_one, r_one)
    return (total[None], jnp.concatenate(chunks, axis=1))


def on_device(e_split, u_one, u_two, *rest):
    width = u_one.shape[2]
    fits = (
        lax.axis_size("seq") == 4
        and lax.axis_size("batch") == 4
        and width == DILATION_FIRST
        and 2 * width == DILATION_SECOND
        and u_one.shape[0] == 1
    )
    return (four_shards if fits else general)(e_split, u_one, u_two, *rest)


def solution(mesh):
    in_specs = (
        P(("grp", "batch"), "seq", None),
        P(("grp", "batch"), None, "seq"),
        P(("grp", "batch"), None, "seq"),
        P(),
        P(),
        P(),
        P(),
    )
    out_specs = (P(("grp", "batch"), None, "seq"), P(("grp", "seq"), None))
    return jax.shard_map(
        on_device, mesh=mesh, in_specs=in_specs, out_specs=out_specs, check_vma=False
    )
```

```python
import math

import jax
import jax.numpy as jnp
from jax import lax
from jax.experimental import pallas as pl
from jax.experimental.pallas import tpu as pltpu
from jax.sharding import PartitionSpec as P

DILATION_FIRST = 512
DILATION_SECOND = 1024


EPS = 1e-06
SLOPE = math.sqrt(2.0 / math.pi)
CUBIC = 0.044715
F32 = jnp.float32
BF16 = jnp.bfloat16
CUTS = (0, 512, 768)


def shifted(value, axis, steps):
    count = lax.axis_size(axis)
    initial, last = (max(0, -steps), min(count, count - steps))
    return lax.ppermute(value, axis, [(source, source + steps) for source in range(initial, last)])


def gelu_slope(normed):
    inner = jnp.tanh(SLOPE * (normed + CUBIC * normed * normed * normed))
    return 0.5 * (1.0 + inner) + 0.5 * normed * (1.0 - inner * inner) * SLOPE * (
        1.0 + 3.0 * CUBIC * normed * normed
    )


def prepare(inputs, gain_vec):
    xfloat = inputs.astype(F32)
    meansq = jnp.mean(xfloat * xfloat, axis=1, keepdims=True)
    scale = lax.rsqrt(meansq + EPS)
    normed = xfloat * scale * gain_vec[None, :, None]
    gelu_out = jax.nn.gelu(normed, approximate=True).astype(BF16)
    return (xfloat, scale, normed, gelu_out)


def input_grad(xfloat, scale, normed, gain_vec, weight, grad_out, grad_upper, grad_lower):
    dgelu = jnp.einsum("co,sop->scp", weight[0], grad_upper, preferred_element_type=F32)
    dgelu = dgelu + jnp.einsum("co,sop->scp", weight[1], grad_out, preferred_element_type=F32)
    dgelu = dgelu + jnp.einsum("co,sop->scp", weight[2], grad_lower, preferred_element_type=F32)
    dnorm = dgelu * gelu_slope(normed) * gain_vec[None, :, None]
    inner = jnp.mean(dnorm * xfloat, axis=1, keepdims=True)
    dinput = scale * dnorm - xfloat * scale * scale * scale * inner
    return (grad_out.astype(F32) + dinput).astype(BF16)


def general(e_split, u_one, u_two, w_one, w_two, c_one, c_two):
    width = u_one.shape[2]
    factor = 1.0 / math.sqrt(
        u_one.shape[0] * lax.axis_size("batch") * width * lax.axis_size("seq")
    )
    e_two = lax.all_to_all(e_split, "seq", split_axis=2, concat_axis=1, tiled=True)
    span = DILATION_SECOND // width
    lower, upper = shifted(e_two, "seq", span), shifted(e_two, "seq", -span)
    xfloat, scale, normed, _ = prepare(u_two, c_two)
    e_one = input_grad(xfloat, scale, normed, c_two, w_two, e_two, upper, lower)
    span = DILATION_FIRST // width
    lower, upper = shifted(e_one, "seq", span), shifted(e_one, "seq", -span)
    xfloat, scale, normed, gelu_out = prepare(u_one, c_one)
    total = input_grad(xfloat, scale, normed, c_one, w_one, e_one, upper, lower)
    pieces = [
        jnp.einsum("scp,sop->co", gelu_out, tapped, preferred_element_type=F32)
        for tapped in (upper, e_one, lower)
    ]
    terms = jnp.concatenate(pieces, axis=0) * factor
    rows = lax.psum_scatter(terms, "seq", scatter_dimension=0, tiled=True)
    return (total, lax.psum(rows, "batch"))


MIB = 1 << 20


def vmem():
    return pl.BlockSpec(memory_space=pltpu.VMEM)


def scalars():
    return pl.BlockSpec(memory_space=pltpu.SMEM)


def cut(e_split, place, width):
    part = e_split.shape[0]
    peers = (3, 2, 1, 0)

    def body(place_ref, e_ref, *rest):
        outs, sems = rest[:4], rest[4]
        me = place_ref[0]
        copies = []
        for n, k in enumerate(peers):
            for j in range(2):
                at = pl.multiple_of((me ^ k ^ (2 * j)) * width, width)
                copies.append(
                    pltpu.make_async_copy(
                        e_ref.at[:, pl.ds(at, width)], outs[n].at[j], sems.at[2 * n + j]
                    )
                )
        for copy in copies:
            copy.start()
        for copy in copies:
            copy.wait()

    return pl.pallas_call(
        body,
        in_specs=[scalars(), pl.BlockSpec(memory_space=pltpu.HBM)],
        out_specs=[vmem()] * 4,
        out_shape=[pltpu.VMEM((2, part, width), BF16)] * 4,
        scratch_shapes=[pltpu.SemaphoreType.DMA((8,))],
        cost_estimate=pl.CostEstimate(
            flops=0, bytes_accessed=32 * part * width, transcendentals=0
        ),
        compiler_params=pltpu.CompilerParams(vmem_limit_bytes=4 * MIB),
        name="cut",
    )(place, e_split)


def prep(u_two, c_two, u_one, c_one):
    chans, width = u_one.shape
    tile = 128
    wide, row = pltpu.VMEM((chans, width), F32), pltpu.VMEM((1, width), F32)
    copy = pltpu.VMEM((chans, width), BF16)

    def layer(u_ref, c_ref, q_ref, r_ref, v_ref, g_ref):
        c = c_ref[...]
        for t in range(width // tile):
            cols = slice(t * tile, (t + 1) * tile)
            v_ref[:, cols] = u_ref[:, cols]
            u = u_ref[:, cols].astype(F32)
            r = lax.rsqrt(jnp.mean(u * u, axis=0, keepdims=True) + EPS)
            a = u * r * c
            inner = jnp.tanh(SLOPE * (a + CUBIC * a * a * a))
            slope = 0.5 * (1.0 + inner) + 0.5 * a * (1.0 - inner * inner) * SLOPE * (
                1.0 + 3.0 * CUBIC * a * a
            )
            q_ref[:, cols] = slope * c
            r_ref[:, cols] = r
            if g_ref is not None:
                g_ref[:, cols] = (0.5 * a * (1.0 + inner)).astype(BF16)

    def body(u2, c2, u1, c1, q2, r2, v2, q1, r1, v1, g1):
        layer(u2, c2, q2, r2, v2, None)
        layer(u1, c1, q1, r1, v1, g1)

    return pl.pallas_call(
        body,
        in_specs=[vmem()] * 4,
        out_specs=[vmem()] * 7,
        out_shape=[wide, row, copy, wide, row, copy, copy],
        cost_estimate=pl.CostEstimate(
            flops=60 * chans * width,
            bytes_accessed=16 * chans * width,
            transcendentals=2 * chans * width,
        ),
        compiler_params=pltpu.CompilerParams(vmem_limit_bytes=8 * MIB),
        name="prep",
    )(u_two, c_two.reshape(chans, 1), u_one, c_one.reshape(chans, 1))


def finish(acc, e, u, q, r):
    dn = acc * q
    mean = jnp.mean(dn * u, axis=0, keepdims=True)
    return e + r * dn - u * (r * r * r * mean)


def middle(pieces, w, u, q, r, place, cuts):
    chans, width = u.shape
    part = pieces[0].shape[1]
    chunks = len(cuts) - 1
    tile = 256

    def body(place_ref, p0, p1, p2, p3, w_ref, u_ref, q_ref, r_ref, *rest):
        outs, e_s = rest[:chunks], rest[chunks]
        me = place_ref[0]
        tap = place_ref[1]
        for k, piece in enumerate((p0, p1, p2, p3)):
            at = pl.multiple_of((me ^ k) * part, part)
            for j in range(2):
                e_s[j, pl.ds(at, part), :] = piece[j]
        for t in range(width // tile):
            cols = slice(t * tile, (t + 1) * tile)
            e = e_s[0, :, cols]
            acc = jnp.dot(w_ref[1], e, preferred_element_type=F32)
            acc = acc + jnp.dot(w_ref[tap], e_s[1, :, cols], preferred_element_type=F32)
            out = finish(
                acc, e.astype(F32), u_ref[:, cols].astype(F32), q_ref[:, cols], r_ref[:, cols]
            ).astype(BF16)
            for n in range(chunks):
                outs[n][:, cols] = out[cuts[n] : cuts[n + 1]]

    return pl.pallas_call(
        body,
        in_specs=[scalars()] + [vmem()] * 8,
        out_specs=[vmem()] * chunks,
        out_shape=[pltpu.VMEM((b - a, width), BF16) for a, b in zip(cuts, cuts[1:])],
        scratch_shapes=[pltpu.VMEM((2, chans, width), BF16)],
        cost_estimate=pl.CostEstimate(
            flops=4 * chans * chans * width, bytes_accessed=10 * chans * width, transcendentals=0
        ),
        compiler_params=pltpu.CompilerParams(vmem_limit_bytes=10 * MIB),
        name="middle",
    )(place, *pieces, w, u, q, r)


def segments(tap, chans, block):
    cuts, row = [], tap * chans
    while row < (tap + 1) * chans:
        end = min((row // block + 1) * block, (tap + 1) * chans)
        cuts.append((row - tap * chans, end - row))
        row = end
    return cuts


def taps(g, own, near, far, place, factor, seq):
    chans, width = g.shape
    block = 3 * chans // seq
    outer = own is None
    sources = [near, far] if outer else list(own)
    sizes = [source.shape[0] for source in sources]
    cols = sizes[0] if outer else sum(sizes)
    kinds = (0, 2) if outer else (1,)
    rows = chans // 4

    def body(place_ref, g_ref, *refs):
        e_refs, (keep_ref, send_ref, acc_s, sem) = refs[:2], refs[2:]
        core = place_ref[2]
        g_all = g_ref[...]
        if outer:
            even = place_ref[3] == 0
            a, b = e_refs[0][...], e_refs[1][...]
            jobs = [(0, 0, 0, jnp.where(even, a, b)), (1, 2, 0, jnp.where(even, b, a))]
        else:
            jobs = [(0, 1, sum(sizes[:n]), ref[...]) for n, ref in enumerate(e_refs)]
        for slot, tap, col, e in jobs:
            acc = lax.dot_general(
                g_all, e, (((1,), (1,)), ((), ())), preferred_element_type=F32
            )
            acc = acc * factor
            base = slot * rows
            for start, length in segments(tap, chans, block):
                part = length // 4
                for q in range(4):
                    row = start + q * part
                    acc_s[q // 2, q % 2, base : base + part, col : col + e.shape[0]] = acc[
                        row : row + part
                    ]
                base += part
        copy = pltpu.make_async_copy(acc_s.at[core], keep_ref, sem)
        copy.start()
        send_ref[...] = acc_s[1 - core].astype(BF16)
        copy.wait()

    shape = (2, rows * len(kinds), cols)
    return pl.pallas_call(
        body,
        in_specs=[scalars()] + [vmem()] * 3,
        out_specs=[vmem(), vmem()],
        out_shape=[pltpu.VMEM(shape, F32), pltpu.VMEM(shape, BF16)],
        scratch_shapes=[pltpu.VMEM((2,) + shape, F32), pltpu.SemaphoreType.DMA],
        cost_estimate=pl.CostEstimate(
            flops=2 * len(kinds) * chans * cols * width,
            bytes_accessed=4 * len(kinds) * chans * cols,
            transcendentals=0,
        ),
        compiler_params=pltpu.CompilerParams(vmem_limit_bytes=14 * MIB),
    )(place, g, *sources)


def assemble(chunks, place):
    rows = chunks[0][0].shape[0]
    cuts = [0]
    for chunk in chunks:
        cuts.append(cuts[-1] + chunk[0].shape[1])
    grain = 48
    grains = rows // grain

    def body(place_ref, *refs):
        out_ref = refs[-1]
        core, x, first = place_ref[2], place_ref[4], place_ref[5]
        for n in range(len(chunks)):
            for k, ref in enumerate(refs[4 * n : 4 * n + 4]):
                q = 2 * (core ^ (k // 2)) + (x ^ (k % 2))
                for j in range(grains):
                    dest = jnp.where(
                        j < first, first * q + j, 4 * first + (grains - first) * q + j - first
                    )
                    at = pl.multiple_of(dest * grain, grain)
                    out_ref[pl.ds(at, grain), cuts[n] : cuts[n + 1]] = ref[
                        j * grain : (j + 1) * grain
                    ].astype(F32)

    return pl.pallas_call(
        body,
        in_specs=[scalars()] + [vmem()] * (4 * len(chunks)),
        out_specs=vmem(),
        out_shape=jax.ShapeDtypeStruct((4 * rows, cuts[-1]), F32),
        compiler_params=pltpu.CompilerParams(vmem_limit_bytes=8 * MIB),
        name="assemble",
    )(place, *[value for chunk in chunks for value in chunk])


def last(owns, nears, fars, w, u, q, r, place):
    chans, width = u.shape
    chunks = len(owns)
    tile = 256

    def body(place_ref, *refs):
        e_refs = refs[: 3 * chunks]
        w_ref, u_ref, q_ref, r_ref, out_ref = refs[3 * chunks :]
        tap = 2 * place_ref[3]
        for t in range(width // tile):
            cols = slice(t * tile, (t + 1) * tile)
            acc = jnp.zeros((chans, tile), F32)
            for n, k in enumerate((1, tap, 2 - tap)):
                e = jnp.concatenate(
                    [ref[:, cols] for ref in e_refs[n * chunks : (n + 1) * chunks]], axis=0
                )
                if n == 0:
                    own = e.astype(F32)
                acc = acc + jnp.dot(w_ref[k], e, preferred_element_type=F32)
            out_ref[:, cols] = finish(
                acc, own, u_ref[:, cols].astype(F32), q_ref[:, cols], r_ref[:, cols]
            ).astype(BF16)

    return pl.pallas_call(
        body,
        in_specs=[scalars()] + [vmem()] * (3 * chunks + 4),
        out_specs=vmem(),
        out_shape=jax.ShapeDtypeStruct((chans, width), BF16),
        cost_estimate=pl.CostEstimate(
            flops=6 * chans * chans * width, bytes_accessed=12 * chans * width, transcendentals=0
        ),
        compiler_params=pltpu.CompilerParams(vmem_limit_bytes=10 * MIB),
        name="last",
    )(place, *owns, *nears, *fars, w, u, q, r)


def glue(body, outs, *args):
    moved_bytes = sum(a.size * a.dtype.itemsize for a in args)
    return pl.pallas_call(
        body,
        in_specs=[scalars()] + [vmem()] * (len(args) - 1),
        out_specs=[vmem()] * len(outs),
        out_shape=[pltpu.VMEM(*out) for out in outs],
        cost_estimate=pl.CostEstimate(flops=0, bytes_accessed=moved_bytes, transcendentals=0),
        compiler_params=pltpu.CompilerParams(vmem_limit_bytes=4 * MIB),
    )(*args)


def after_core(keep, far, place):
    shape = keep.shape[1:]

    def body(place_ref, keep_ref, far_ref, own_ref, send_ref):
        x = place_ref[4]
        own_ref[...] = keep_ref[x] + far_ref[x].astype(F32)
        send_ref[...] = (keep_ref[1 - x] + far_ref[1 - x].astype(F32)).astype(BF16)

    return glue(body, [(shape, F32), (shape, BF16)], place, keep, far)


def after_x(outer, far, center, far_center, columns, seq, place):
    rows, cols = outer.shape
    third = rows // 2
    unit = 3 * third // seq

    def body(place_ref, a_ref, fa_ref, b_ref, fb_ref, keep_ref, send_ref, part_s):
        me = place_ref[0]
        for tap in range(3):
            if tap == 1:
                value = b_ref[:, columns] + fb_ref[:, columns].astype(F32)
            else:
                at = slice(tap // 2 * third, (tap // 2 + 1) * third)
                value = a_ref[at] + fa_ref[at].astype(F32)
            row = tap * third
            while row < (tap + 1) * third:
                end = min((row // unit + 1) * unit, (tap + 1) * third)
                base = row // unit * unit
                part_s[row // unit, row - base : end - base] = value[
                    row - tap * third : end - tap * third
                ]
                row = end
        for n in range(2):
            keep_ref[n] = part_s[me ^ (2 * n)]
            send_ref[n] = part_s[me ^ (2 * n + 1)].astype(BF16)

    shape = (2, unit, cols)
    args = (place, outer, far, center, far_center)
    return pl.pallas_call(
        body,
        in_specs=[scalars()] + [vmem()] * 4,
        out_specs=[vmem()] * 2,
        out_shape=[pltpu.VMEM(shape, F32), pltpu.VMEM(shape, BF16)],
        scratch_shapes=[pltpu.VMEM((seq, unit, cols), F32)],
        cost_estimate=pl.CostEstimate(
            flops=0, bytes_accessed=12 * seq * unit * cols, transcendentals=0
        ),
        compiler_params=pltpu.CompilerParams(vmem_limit_bytes=6 * MIB),
    )(*args)


def after_near(keep, near, place):
    shape = keep.shape[1:]

    def body(place_ref, keep_ref, near_ref, own_ref, send_ref):
        own_ref[...] = keep_ref[0] + near_ref[0].astype(F32)
        send_ref[...] = (keep_ref[1] + near_ref[1].astype(F32)).astype(BF16)

    return glue(body, [(shape, F32), (shape, BF16)], place, keep, near)


def after_far(own, far, place):
    def body(place_ref, own_ref, far_ref, out_ref):
        out_ref[...] = (own_ref[...] + far_ref[...].astype(F32)).astype(BF16)

    return glue(body, [(own.shape, BF16)], place, own, far)[0]


def pairs(count, flip):
    return [(i, i ^ flip) for i in range(count)]


def four_shards(e_split, u_one, u_two, w_one, w_two, c_one, c_two):
    seq, batch = lax.axis_size("seq"), lax.axis_size("batch")
    me = lax.axis_index("seq")
    core, x = lax.axis_index("batch") % 2, lax.axis_index("batch") // 2
    e_split, u_one, u_two = e_split[0], u_one[0], u_two[0]
    chans, width = u_one.shape
    factor = 1.0 / math.sqrt(batch * width * seq)
    block = 3 * chans // seq
    first = jnp.minimum(block, chans - (block * me) % chans) // (4 * 48)
    place = jnp.stack([me, jnp.where(me < 2, 0, 2), core, me % 2, x, first]).astype(jnp.int32)

    three, two, one, own = cut(e_split, place, width)
    three = lax.ppermute(three, "seq", pairs(seq, 3))
    two = lax.ppermute(two, "seq", pairs(seq, 2))
    one = lax.ppermute(one, "seq", pairs(seq, 1))
    q_two, r_two, v_two, q_one, r_one, v_one, g_one = prep(u_two, c_two, u_one, c_one)
    owns = middle((own, one, two, three), w_two, v_two, q_two, r_two, place, CUTS)
    nears = [lax.ppermute(e, "seq", pairs(seq, 1)) for e in owns]
    fars = [lax.ppermute(e, "seq", [(1, 2), (2, 1)]) for e in owns]

    def over_batch(own, near, far):
        keep, send = taps(g_one, own, near, far, place, factor, seq)
        send = lax.ppermute(send, "batch", pairs(batch, 1))
        keep, send = after_core(keep, send, place)
        return keep, lax.ppermute(send, "batch", pairs(batch, 2))

    center = over_batch(owns, None, None)
    chunks = []
    for j in range(len(owns)):
        outer = over_batch(None, nears[j], fars[j])
        columns = slice(CUTS[j], CUTS[j + 1])
        keep, send = after_x(*outer, *center, columns, seq, place)
        near = lax.ppermute(send, "seq", pairs(seq, 1))
        keep, send = after_near(keep, near, place)
        far = lax.ppermute(send, "seq", pairs(seq, 2))
        mine = after_far(keep, far, place)
        over_x = lax.ppermute(mine, "batch", pairs(batch, 2))
        over_core = lax.ppermute(mine, "batch", pairs(batch, 1))
        over_both = lax.ppermute(over_x, "batch", pairs(batch, 1))
        chunks.append((mine, over_x, over_core, over_both))
    gradient = assemble(chunks, place)
    total = last(owns, nears, fars, w_one, v_one, q_one, r_one, place)
    return (total[None], gradient)


def fits(sizes, width, samples):
    return (
        sizes["seq"] == 4
        and sizes["batch"] == 4
        and width == DILATION_FIRST
        and 2 * width == DILATION_SECOND
        and samples == 1
    )


def on_device(e_split, u_one, u_two, *rest):
    sizes = {name: lax.axis_size(name) for name in ("seq", "batch")}
    if not fits(sizes, u_one.shape[2], u_one.shape[0]):
        return general(e_split, u_one, u_two, *rest)
    return four_shards(e_split, u_one, u_two, *rest)


def solution(mesh):
    in_specs = (
        P(("grp", "batch"), "seq", None),
        P(("grp", "batch"), None, "seq"),
        P(("grp", "batch"), None, "seq"),
        P(),
        P(),
        P(),
        P(),
    )
    out_specs = (P(("grp", "batch"), None, "seq"), P(("grp", "seq"), None))
    return jax.shard_map(
        on_device, mesh=mesh, in_specs=in_specs, out_specs=out_specs, check_vma=False
    )
```

```python
import math

import jax
import jax.numpy as jnp
from jax import lax
from jax.experimental import pallas as pl
from jax.experimental.pallas import tpu as pltpu
from jax.sharding import PartitionSpec as P

DILATION_FIRST = 512
DILATION_SECOND = 1024


EPS = 1e-06
SLOPE = math.sqrt(2.0 / math.pi)
CUBIC = 0.044715
F32 = jnp.float32
BF16 = jnp.bfloat16
SPLITS = ((384,), (256,), (128,))
CUTS = (0, 384, 640, 768)


def shifted(value, axis, steps):
    count = lax.axis_size(axis)
    initial, last = (max(0, -steps), min(count, count - steps))
    return lax.ppermute(value, axis, [(source, source + steps) for source in range(initial, last)])


def gelu_slope(normed):
    inner = jnp.tanh(SLOPE * (normed + CUBIC * normed * normed * normed))
    return 0.5 * (1.0 + inner) + 0.5 * normed * (1.0 - inner * inner) * SLOPE * (
        1.0 + 3.0 * CUBIC * normed * normed
    )


def prepare(inputs, gain_vec):
    xfloat = inputs.astype(F32)
    meansq = jnp.mean(xfloat * xfloat, axis=1, keepdims=True)
    scale = lax.rsqrt(meansq + EPS)
    normed = xfloat * scale * gain_vec[None, :, None]
    gelu_out = jax.nn.gelu(normed, approximate=True).astype(BF16)
    return (xfloat, scale, normed, gelu_out)


def input_grad(xfloat, scale, normed, gain_vec, weight, grad_out, grad_upper, grad_lower):
    dgelu = jnp.einsum("co,sop->scp", weight[0], grad_upper, preferred_element_type=F32)
    dgelu = dgelu + jnp.einsum("co,sop->scp", weight[1], grad_out, preferred_element_type=F32)
    dgelu = dgelu + jnp.einsum("co,sop->scp", weight[2], grad_lower, preferred_element_type=F32)
    dnorm = dgelu * gelu_slope(normed) * gain_vec[None, :, None]
    inner = jnp.mean(dnorm * xfloat, axis=1, keepdims=True)
    dinput = scale * dnorm - xfloat * scale * scale * scale * inner
    return (grad_out.astype(F32) + dinput).astype(BF16)


def general(e_split, u_one, u_two, w_one, w_two, c_one, c_two):
    width = u_one.shape[2]
    factor = 1.0 / math.sqrt(
        u_one.shape[0] * lax.axis_size("batch") * width * lax.axis_size("seq")
    )
    e_two = lax.all_to_all(e_split, "seq", split_axis=2, concat_axis=1, tiled=True)
    span = DILATION_SECOND // width
    lower, upper = shifted(e_two, "seq", span), shifted(e_two, "seq", -span)
    xfloat, scale, normed, _ = prepare(u_two, c_two)
    e_one = input_grad(xfloat, scale, normed, c_two, w_two, e_two, upper, lower)
    span = DILATION_FIRST // width
    lower, upper = shifted(e_one, "seq", span), shifted(e_one, "seq", -span)
    xfloat, scale, normed, gelu_out = prepare(u_one, c_one)
    total = input_grad(xfloat, scale, normed, c_one, w_one, e_one, upper, lower)
    pieces = [
        jnp.einsum("scp,sop->co", gelu_out, tapped, preferred_element_type=F32)
        for tapped in (upper, e_one, lower)
    ]
    terms = jnp.concatenate(pieces, axis=0) * factor
    rows = lax.psum_scatter(terms, "seq", scatter_dimension=0, tiled=True)
    return (total, lax.psum(rows, "batch"))


MIB = 1 << 20


def vmem():
    return pl.BlockSpec(memory_space=pltpu.VMEM)


def scalars():
    return pl.BlockSpec(memory_space=pltpu.SMEM)


def cut(e_split, place, width):
    part = e_split.shape[0]
    peers = (3, 2, 1, 0)

    def body(place_ref, e_ref, *rest):
        outs, sems = rest[:4], rest[4]
        me = place_ref[0]
        copies = []
        for n, k in enumerate(peers):
            for j in range(2):
                at = pl.multiple_of((me ^ k ^ (2 * j)) * width, width)
                copies.append(
                    pltpu.make_async_copy(
                        e_ref.at[:, pl.ds(at, width)], outs[n].at[j], sems.at[2 * n + j]
                    )
                )
        for copy in copies:
            copy.start()
        for copy in copies:
            copy.wait()

    return pl.pallas_call(
        body,
        in_specs=[scalars(), pl.BlockSpec(memory_space=pltpu.HBM)],
        out_specs=[vmem()] * 4,
        out_shape=[pltpu.VMEM((2, part, width), BF16)] * 4,
        scratch_shapes=[pltpu.SemaphoreType.DMA((8,))],
        cost_estimate=pl.CostEstimate(
            flops=0, bytes_accessed=32 * part * width, transcendentals=0
        ),
        compiler_params=pltpu.CompilerParams(vmem_limit_bytes=4 * MIB),
        name="cut",
    )(place, e_split)


def prep(u_two, c_two, u_one, c_one):
    chans, width = u_one.shape
    tile = 128
    wide, row = pltpu.VMEM((chans, width), F32), pltpu.VMEM((1, width), F32)
    copy = pltpu.VMEM((chans, width), BF16)

    def layer(u_ref, c_ref, q_ref, r_ref, v_ref, g_ref):
        c = c_ref[...]
        for t in range(width // tile):
            cols = slice(t * tile, (t + 1) * tile)
            v_ref[:, cols] = u_ref[:, cols]
            u = u_ref[:, cols].astype(F32)
            r = lax.rsqrt(jnp.mean(u * u, axis=0, keepdims=True) + EPS)
            a = u * r * c
            inner = jnp.tanh(SLOPE * (a + CUBIC * a * a * a))
            slope = 0.5 * (1.0 + inner) + 0.5 * a * (1.0 - inner * inner) * SLOPE * (
                1.0 + 3.0 * CUBIC * a * a
            )
            q_ref[:, cols] = slope * c
            r_ref[:, cols] = r
            if g_ref is not None:
                g_ref[:, cols] = (0.5 * a * (1.0 + inner)).astype(BF16)

    def body(u2, c2, u1, c1, q2, r2, v2, q1, r1, v1, g1):
        layer(u2, c2, q2, r2, v2, None)
        layer(u1, c1, q1, r1, v1, g1)

    return pl.pallas_call(
        body,
        in_specs=[vmem()] * 4,
        out_specs=[vmem()] * 7,
        out_shape=[wide, row, copy, wide, row, copy, copy],
        cost_estimate=pl.CostEstimate(
            flops=60 * chans * width,
            bytes_accessed=16 * chans * width,
            transcendentals=2 * chans * width,
        ),
        compiler_params=pltpu.CompilerParams(vmem_limit_bytes=8 * MIB),
        name="prep",
    )(u_two, c_two.reshape(chans, 1), u_one, c_one.reshape(chans, 1))


def finish(acc, e, u, q, r):
    dn = acc * q
    mean = jnp.mean(dn * u, axis=0, keepdims=True)
    return e + r * dn - u * (r * r * r * mean)


def middle(pieces, w, u, q, r, place, cuts):
    chans, width = u.shape
    part = pieces[0].shape[1]
    chunks = len(cuts) - 1
    tile = 256

    def body(place_ref, p0, p1, p2, p3, w_ref, u_ref, q_ref, r_ref, *rest):
        outs, e_s = rest[:chunks], rest[chunks]
        me = place_ref[0]
        tap = place_ref[1]
        for k, piece in enumerate((p0, p1, p2, p3)):
            at = pl.multiple_of((me ^ k) * part, part)
            for j in range(2):
                e_s[j, pl.ds(at, part), :] = piece[j]
        for t in range(width // tile):
            cols = slice(t * tile, (t + 1) * tile)
            e = e_s[0, :, cols]
            acc = jnp.dot(w_ref[1], e, preferred_element_type=F32)
            acc = acc + jnp.dot(w_ref[tap], e_s[1, :, cols], preferred_element_type=F32)
            out = finish(
                acc, e.astype(F32), u_ref[:, cols].astype(F32), q_ref[:, cols], r_ref[:, cols]
            ).astype(BF16)
            for n in range(chunks):
                outs[n][:, cols] = out[cuts[n] : cuts[n + 1]]

    return pl.pallas_call(
        body,
        in_specs=[scalars()] + [vmem()] * 8,
        out_specs=[vmem()] * chunks,
        out_shape=[pltpu.VMEM((b - a, width), BF16) for a, b in zip(cuts, cuts[1:])],
        scratch_shapes=[pltpu.VMEM((2, chans, width), BF16)],
        cost_estimate=pl.CostEstimate(
            flops=4 * chans * chans * width, bytes_accessed=10 * chans * width, transcendentals=0
        ),
        compiler_params=pltpu.CompilerParams(vmem_limit_bytes=10 * MIB),
        name="middle",
    )(place, *pieces, w, u, q, r)


def segments(tap, chans, block):
    cuts, row = [], tap * chans
    while row < (tap + 1) * chans:
        end = min((row // block + 1) * block, (tap + 1) * chans)
        cuts.append((row - tap * chans, end - row))
        row = end
    return cuts


def taps(g, own, near, far, place, factor, seq):
    chans, width = g.shape
    block = 3 * chans // seq
    outer = own is None
    sources = [near, far] if outer else list(own)
    sizes = [source.shape[0] for source in sources]
    cols = sizes[0] if outer else sum(sizes)
    kinds = (0, 2) if outer else (1,)
    rows = chans // 4

    def body(place_ref, g_ref, *refs):
        e_refs, (keep_ref, send_ref, acc_s, sem) = refs[: len(sources)], refs[len(sources) :]
        core = place_ref[2]
        g_all = g_ref[...]
        if outer:
            even = place_ref[3] == 0
            a, b = e_refs[0][...], e_refs[1][...]
            jobs = [(0, 0, 0, jnp.where(even, a, b)), (1, 2, 0, jnp.where(even, b, a))]
        else:
            jobs = [(0, 1, sum(sizes[:n]), ref[...]) for n, ref in enumerate(e_refs)]
        for slot, tap, col, e in jobs:
            acc = lax.dot_general(
                g_all, e, (((1,), (1,)), ((), ())), preferred_element_type=F32
            )
            acc = acc * factor
            base = slot * rows
            for start, length in segments(tap, chans, block):
                part = length // 4
                for q in range(4):
                    row = start + q * part
                    acc_s[q // 2, q % 2, base : base + part, col : col + e.shape[0]] = acc[
                        row : row + part
                    ]
                base += part
        copy = pltpu.make_async_copy(acc_s.at[core], keep_ref, sem)
        copy.start()
        send_ref[...] = acc_s[1 - core].astype(BF16)
        copy.wait()

    shape = (2, rows * len(kinds), cols)
    return pl.pallas_call(
        body,
        in_specs=[scalars()] + [vmem()] * (1 + len(sources)),
        out_specs=[vmem(), vmem()],
        out_shape=[pltpu.VMEM(shape, F32), pltpu.VMEM(shape, BF16)],
        scratch_shapes=[pltpu.VMEM((2,) + shape, F32), pltpu.SemaphoreType.DMA],
        cost_estimate=pl.CostEstimate(
            flops=2 * len(kinds) * chans * cols * width,
            bytes_accessed=4 * len(kinds) * chans * cols,
            transcendentals=0,
        ),
        compiler_params=pltpu.CompilerParams(vmem_limit_bytes=14 * MIB),
    )(place, g, *sources)


def assemble(shares, column, whole, into, place):
    rows = shares[0][0].shape[0]
    sizes = [share[0].shape[1] for share in shares]
    cols = sum(sizes)
    grain = 48
    grains = rows // grain
    count = 4 * len(shares)

    def body(place_ref, *refs):
        out_ref, out_s, sem = refs[-3:]
        core, x, first = place_ref[2], place_ref[4], place_ref[5]
        for k, ref in enumerate(refs[:count]):
            q = 2 * (core ^ (k % 4 // 2)) + (x ^ (k % 2))
            col = sum(sizes[: k // 4])
            at_cols = slice(col, col + sizes[k // 4])
            for j in range(grains):
                dest = jnp.where(
                    j < first, first * q + j, 4 * first + (grains - first) * q + j - first
                )
                at = pl.multiple_of(dest * grain, grain)
                out_s[pl.ds(at, grain), at_cols] = ref[j * grain : (j + 1) * grain].astype(F32)
        copy = pltpu.make_async_copy(out_s, out_ref.at[:, column : column + cols], sem)
        copy.start()
        copy.wait()

    values = [value for share in shares for value in share]
    extra = [] if into is None else [into]
    hbm = pl.BlockSpec(memory_space=pltpu.HBM)
    return pl.pallas_call(
        body,
        in_specs=[scalars()] + [vmem()] * count + [hbm] * len(extra),
        out_specs=hbm,
        out_shape=jax.ShapeDtypeStruct((4 * rows, whole), F32),
        scratch_shapes=[pltpu.VMEM((4 * rows, cols), F32), pltpu.SemaphoreType.DMA],
        input_output_aliases={count + 1: 0} if extra else {},
        cost_estimate=pl.CostEstimate(
            flops=0, bytes_accessed=24 * rows * cols, transcendentals=0
        ),
        compiler_params=pltpu.CompilerParams(vmem_limit_bytes=6 * MIB),
    )(place, *values, *extra)


def first_taps(owns, nears, fars, start, acc, w, place, tail=None):
    chans, width = w.shape[1], (owns or nears)[0].shape[1]
    tile = 256
    inputs = [*(owns or ()), *(nears or ()), *(fars or ())]
    count = len(inputs)

    def body(place_ref, *refs):
        out_ref = refs[-1]
        e_refs, w_ref, rest = refs[:count], refs[count], refs[count + 1 : -1]
        near_tap = 2 * place_ref[3]
        for t in range(width // tile):
            cols = slice(t * tile, (t + 1) * tile)
            total = rest[0][:, cols] if acc is not None else None
            at = 0
            for group, k in ((owns, 1), (nears, near_tap), (fars, 2 - near_tap)):
                channel = start
                for _ in group or ():
                    e = e_refs[at][:, cols]
                    part = w_ref[k, :, channel : channel + e.shape[0]]
                    value = jnp.dot(part, e, preferred_element_type=F32)
                    total = value if total is None else total + value
                    channel += e.shape[0]
                    at += 1
            if tail is None:
                out_ref[:, cols] = total
                continue
            u_ref, q_ref, r_ref = rest[1:4]
            own = jnp.concatenate([ref[:, cols] for ref in rest[4:]], axis=0)
            out_ref[:, cols] = finish(
                total,
                own.astype(F32),
                u_ref[:, cols].astype(F32),
                q_ref[:, cols],
                r_ref[:, cols],
            ).astype(BF16)

    args = [*inputs, w] + ([] if acc is None else [acc]) + list(tail or ())
    wide = (chans, width)
    return pl.pallas_call(
        body,
        in_specs=[scalars()] + [vmem()] * len(args),
        out_specs=vmem(),
        out_shape=pltpu.VMEM(wide, F32) if tail is None else jax.ShapeDtypeStruct(wide, BF16),
        cost_estimate=pl.CostEstimate(
            flops=2 * chans * width * sum(e.shape[0] for e in inputs),
            bytes_accessed=8 * chans * width,
            transcendentals=0,
        ),
        compiler_params=pltpu.CompilerParams(vmem_limit_bytes=10 * MIB),
    )(place, *args)


def glue(body, outs, *args):
    moved_bytes = sum(a.size * a.dtype.itemsize for a in args)
    return pl.pallas_call(
        body,
        in_specs=[scalars()] + [vmem()] * (len(args) - 1),
        out_specs=[vmem()] * len(outs),
        out_shape=[pltpu.VMEM(*out) for out in outs],
        cost_estimate=pl.CostEstimate(flops=0, bytes_accessed=moved_bytes, transcendentals=0),
        compiler_params=pltpu.CompilerParams(vmem_limit_bytes=4 * MIB),
    )(*args)


def after_core(keep, far, splits, place):
    rows = keep.shape[1]

    def body(place_ref, keep_ref, far_ref, *outs):
        x = place_ref[4]
        col = 0
        for n, size in enumerate(splits):
            at = slice(col, col + size)
            outs[2 * n][...] = keep_ref[x, :, at] + far_ref[x, :, at].astype(F32)
            outs[2 * n + 1][...] = (
                keep_ref[1 - x, :, at] + far_ref[1 - x, :, at].astype(F32)
            ).astype(BF16)
            col += size

    outs = [((rows, size), kind) for size in splits for kind in (F32, BF16)]
    return glue(body, outs, place, keep, far)


def after_x(outer, far, center, far_center, columns, seq, place):
    rows, cols = outer.shape
    third = rows // 2
    unit = 3 * third // seq

    def body(place_ref, a_ref, fa_ref, b_ref, fb_ref, keep_ref, send_ref, part_s):
        me = place_ref[0]
        for tap in range(3):
            if tap == 1:
                value = b_ref[:, columns] + fb_ref[:, columns].astype(F32)
            else:
                at = slice(tap // 2 * third, (tap // 2 + 1) * third)
                value = a_ref[at] + fa_ref[at].astype(F32)
            row = tap * third
            while row < (tap + 1) * third:
                end = min((row // unit + 1) * unit, (tap + 1) * third)
                base = row // unit * unit
                part_s[row // unit, row - base : end - base] = value[
                    row - tap * third : end - tap * third
                ]
                row = end
        for n in range(2):
            keep_ref[n] = part_s[me ^ (2 * n)]
            send_ref[n] = part_s[me ^ (2 * n + 1)].astype(BF16)

    shape = (2, unit, cols)
    args = (place, outer, far, center, far_center)
    return pl.pallas_call(
        body,
        in_specs=[scalars()] + [vmem()] * 4,
        out_specs=[vmem()] * 2,
        out_shape=[pltpu.VMEM(shape, F32), pltpu.VMEM(shape, BF16)],
        scratch_shapes=[pltpu.VMEM((seq, unit, cols), F32)],
        cost_estimate=pl.CostEstimate(
            flops=0, bytes_accessed=12 * seq * unit * cols, transcendentals=0
        ),
        compiler_params=pltpu.CompilerParams(vmem_limit_bytes=6 * MIB),
    )(*args)


def after_near(keep, near, place):
    shape = keep.shape[1:]

    def body(place_ref, keep_ref, near_ref, own_ref, send_ref):
        own_ref[...] = keep_ref[0] + near_ref[0].astype(F32)
        send_ref[...] = (keep_ref[1] + near_ref[1].astype(F32)).astype(BF16)

    return glue(body, [(shape, F32), (shape, BF16)], place, keep, near)


def after_far(own, far, place):
    def body(place_ref, own_ref, far_ref, out_ref):
        out_ref[...] = (own_ref[...] + far_ref[...].astype(F32)).astype(BF16)

    return glue(body, [(own.shape, BF16)], place, own, far)[0]


def pairs(count, flip):
    return [(i, i ^ flip) for i in range(count)]


def four_shards(e_split, u_one, u_two, w_one, w_two, c_one, c_two):
    seq, batch = lax.axis_size("seq"), lax.axis_size("batch")
    me = lax.axis_index("seq")
    core, x = lax.axis_index("batch") % 2, lax.axis_index("batch") // 2
    e_split, u_one, u_two = e_split[0], u_one[0], u_two[0]
    chans, width = u_one.shape
    factor = 1.0 / math.sqrt(batch * width * seq)
    block = 3 * chans // seq
    first = jnp.minimum(block, chans - (block * me) % chans) // (4 * 48)
    place = jnp.stack([me, jnp.where(me < 2, 0, 2), core, me % 2, x, first]).astype(jnp.int32)

    three, two, one, own = cut(e_split, place, width)
    three = lax.ppermute(three, "seq", pairs(seq, 3))
    two = lax.ppermute(two, "seq", pairs(seq, 2))
    one = lax.ppermute(one, "seq", pairs(seq, 1))
    q_two, r_two, v_two, q_one, r_one, v_one, g_one = prep(u_two, c_two, u_one, c_one)
    owns = middle((own, one, two, three), w_two, v_two, q_two, r_two, place, CUTS)
    nears = [lax.ppermute(e, "seq", pairs(seq, 1)) for e in owns]
    fars = [lax.ppermute(e, "seq", [(1, 2), (2, 1)]) for e in owns]

    def over_core(own, near, far, splits):
        keep, send = taps(g_one, own, near, far, place, factor, seq)
        send = lax.ppermute(send, "batch", pairs(batch, 1))
        outs = after_core(keep, send, splits, place)
        return list(zip(outs[::2], outs[1::2]))

    ((center, send),) = over_core(owns, None, None, (chans,))
    far_center = lax.ppermute(send, "batch", pairs(batch, 2))
    parts = []
    for j, splits in enumerate(SPLITS):
        parts += over_core(None, nears[j], fars[j], splits)
    shares, column = [], 0
    for outer, send in parts:
        send = lax.ppermute(send, "batch", pairs(batch, 2))
        end = column + outer.shape[1]
        keep, send = after_x(outer, send, center, far_center, slice(column, end), seq, place)
        near = lax.ppermute(send, "seq", pairs(seq, 1))
        keep, send = after_near(keep, near, place)
        far = lax.ppermute(send, "seq", pairs(seq, 2))
        mine = after_far(keep, far, place)
        over_x = lax.ppermute(mine, "batch", pairs(batch, 2))
        over_core_ = lax.ppermute(mine, "batch", pairs(batch, 1))
        over_both = lax.ppermute(over_x, "batch", pairs(batch, 1))
        shares.append((mine, over_x, over_core_, over_both))
        column = end
    first_column = shares[0][0].shape[1]
    gradient = assemble(shares[:1], 0, chans, None, place)
    gradient = assemble(shares[1:], first_column, chans, gradient, place)
    total = first_taps(owns, None, None, 0, None, w_one, place)
    for j in range(len(owns)):
        tail = (v_one, q_one, r_one, *owns) if j == len(owns) - 1 else None
        total = first_taps(
            None, nears[j : j + 1], fars[j : j + 1], CUTS[j], total, w_one, place, tail
        )
    return (total[None], gradient)


def fits(sizes, width, samples):
    return (
        sizes["seq"] == 4
        and sizes["batch"] == 4
        and width == DILATION_FIRST
        and 2 * width == DILATION_SECOND
        and samples == 1
    )


def on_device(e_split, u_one, u_two, *rest):
    sizes = {name: lax.axis_size(name) for name in ("seq", "batch")}
    if not fits(sizes, u_one.shape[2], u_one.shape[0]):
        return general(e_split, u_one, u_two, *rest)
    return four_shards(e_split, u_one, u_two, *rest)


def solution(mesh):
    in_specs = (
        P(("grp", "batch"), "seq", None),
        P(("grp", "batch"), None, "seq"),
        P(("grp", "batch"), None, "seq"),
        P(),
        P(),
        P(),
        P(),
    )
    out_specs = (P(("grp", "batch"), None, "seq"), P(("grp", "seq"), None))
    return jax.shard_map(
        on_device, mesh=mesh, in_specs=in_specs, out_specs=out_specs, check_vma=False
    )
```
